512 devices in a mesh: ctx: 128 (over y, x_lo, z), head: 4 (over x_hi, core).
Axes of the slice: x: 4 (x_hi: 2, x_lo: 2; x = x_hi * 2 + x_lo), y: 8, z: 8, core: 2. Of those that a mesh axis runs over, the one named last changes fastest.
Arguments:
- query_proj: bfloat16 [16384, 4096], P(('ctx', 'head')), may hold values from -6 to 6
- key_proj: bfloat16 [16384, 2048], P(('ctx', 'head')), may hold values from -6 to 6
- value_proj: bfloat16 [16384, 2048], P(('ctx', 'head')), may hold values from -6 to 6
- out_grad: bfloat16 [16384, 4096], P(('ctx', 'head')), may hold values from -6 to 6
Outputs:
- query_grad: bfloat16 [16384, 4096], P(('ctx', 'head'))
- key_grad: bfloat16 [16384, 2048], P(('ctx', 'head'))
- value_grad: bfloat16 [16384, 2048], P(('ctx', 'head'))
The draws below stay inside these ranges and needn't reach their ends.
All inputs are finite; a program needn't handle non-finite values.
Results may differ from the reference program's by a relative error of at most 0.0049.
Values may be sent and summed in bfloat16 or wider, within the bound.
No kernel may reach another device: no remote copies, remote signals or barrier semaphores. Data moves between devices by JAX's collectives and lax.ppermute only.
A program may use at most 64 MiB of HBM per device.

```python
import math
import jax
import jax.numpy as jnp
from jax import lax

HEADS = 16
KV_HEADS = 8
HEAD_DIM = 256
TOK_DEV = 128
WINDOW = 512
TOKENS = 16384


def block_levels(own_key, shape, cuts, smallest, largest):
    def one(position, blocks):
        heights = jax.random.uniform(jax.random.fold_in(jax.random.fold_in(own_key, 6), position), (blocks,), jnp.float32, smallest / len(cuts), largest / len(cuts))
        return jnp.repeat(jnp.exp(heights), shape[position] // blocks).reshape((-1,) + (1,) * (len(shape) - position - 1))

    level = one(*cuts[0])
    for cut in cuts[1:]:
        level = level * one(*cut)
    return level


def bell_draw(rng, dims, spread, most, split=(), held_as=jnp.bfloat16):
    array = spread * jax.random.normal(rng, dims, jnp.float32)
    if split:
        array = array * block_levels(rng, dims, split, -0.22, 0.18)
    return jnp.clip(array, -most, most).astype(held_as)


def setup_inputs(seed: int = 0) -> dict:
    seeds = jax.random.split(jax.random.key(seed), 5)
    return {
        "query_proj": bell_draw(seeds[0], (TOKENS, HEADS * HEAD_DIM), 1.0, 6.0, ((0, 512),)),
        "key_proj": bell_draw(seeds[1], (TOKENS, KV_HEADS * HEAD_DIM), 1.0, 6.0, ((0, 512),)),
        "value_proj": bell_draw(seeds[2], (TOKENS, KV_HEADS * HEAD_DIM), 1.0, 6.0, ((0, 512),)),
        "out_grad": bell_draw(seeds[3], (TOKENS, HEADS * HEAD_DIM), 1.0, 6.0, ((0, 512),)),
    }


SOFTCAP = 50.0

def reference(query_proj, key_proj, value_proj, out_grad):
    token_count = query_proj.shape[0]
    kv_width = key_proj.shape[1]
    kv_heads = KV_HEADS
    group_size = HEADS // KV_HEADS
    window_rows = WINDOW
    block_rows = TOK_DEV
    span_rows = window_rows + block_rows
    score_scale = 1.0 / math.sqrt(HEAD_DIM)
    front = jnp.zeros((window_rows, kv_width), key_proj.dtype)
    keys_pad = jnp.concatenate([front, key_proj], axis=0)
    values_pad = jnp.concatenate([front, value_proj], axis=0)
    highest = lax.Precision.HIGHEST

    def step(carry, index):
        key_acc, value_acc = carry
        start = index * block_rows
        queries = lax.dynamic_slice_in_dim(query_proj, start, block_rows, 0).astype(jnp.float32)
        queries = queries.reshape(block_rows, kv_heads, group_size, HEAD_DIM)
        grads_out = lax.dynamic_slice_in_dim(out_grad, start, block_rows, 0).astype(jnp.float32)
        grads_out = grads_out.reshape(block_rows, kv_heads, group_size, HEAD_DIM)
        keys_win = lax.dynamic_slice_in_dim(keys_pad, start, span_rows, 0).astype(jnp.float32)
        keys_win = keys_win.reshape(span_rows, kv_heads, HEAD_DIM)
        values_win = lax.dynamic_slice_in_dim(values_pad, start, span_rows, 0).astype(jnp.float32)
        values_win = values_win.reshape(span_rows, kv_heads, HEAD_DIM)
        query_pos = start + jnp.arange(block_rows, dtype=jnp.int32)
        key_pos = start - window_rows + jnp.arange(span_rows, dtype=jnp.int32)
        offset = query_pos[:, None] - key_pos[None, :]
        allowed = (offset >= 0) & (offset < window_rows) & (key_pos >= 0)[None, :]
        raw_scores = jnp.einsum('tgnd,sgd->gnts', queries, keys_win, precision=highest)
        capped = SOFTCAP * jnp.tanh(raw_scores * score_scale / SOFTCAP)
        exp_total = lax.optimization_barrier(jnp.sum(jnp.where(allowed, jnp.exp(capped), jnp.float32(0.0)), axis=-1))
        log_total = jnp.log(exp_total)
        attn_weights = jnp.where(allowed, jnp.exp(capped - log_total[..., None]), jnp.float32(0.0))
        dweights = jnp.einsum('tgnd,sgd->gnts', grads_out, values_win, precision=highest)
        row_delta = lax.optimization_barrier(jnp.sum(attn_weights * dweights, axis=-1))
        dscores = (attn_weights * (dweights - row_delta[..., None]) * (1.0 - capped * capped / (SOFTCAP * SOFTCAP)) * score_scale).astype(jnp.bfloat16)
        weights_low = attn_weights.astype(jnp.bfloat16)
        dscores, weights_low = lax.optimization_barrier((dscores, weights_low))
        dscores_wide = dscores.astype(jnp.float32)
        weights_wide = weights_low.astype(jnp.float32)
        query_block = jnp.einsum('gnts,sgd->tgnd', dscores_wide, keys_win, precision=highest)
        query_block = query_block.reshape(block_rows, -1).astype(jnp.bfloat16)
        key_part = jnp.einsum('gnts,tgnd->sgd', dscores_wide, queries, precision=highest).reshape(span_rows, kv_width)
        value_part = jnp.einsum('gnts,tgnd->sgd', weights_wide, grads_out, precision=highest).reshape(span_rows, kv_width)
        key_acc = lax.dynamic_update_slice_in_dim(key_acc, lax.dynamic_slice_in_dim(key_acc, start, span_rows, 0) + key_part, start, 0)
        value_acc = lax.dynamic_update_slice_in_dim(value_acc, lax.dynamic_slice_in_dim(value_acc, start, span_rows, 0) + value_part, start, 0)
        return ((key_acc, value_acc), query_block)
    indices = jnp.arange(token_count // block_rows, dtype=jnp.int32)
    zeros_acc = jnp.zeros((token_count + window_rows, kv_width), jnp.float32)
    (key_acc, value_acc), blocks = lax.scan(step, (zeros_acc, zeros_acc), indices)
    query_grad = blocks.reshape(token_count, -1)
    key_grad = key_acc[window_rows:].astype(jnp.bfloat16)
    value_grad = value_acc[window_rows:].astype(jnp.bfloat16)
    return (query_grad, key_grad, value_grad)
```

```python
import math

import jax
import jax.numpy as jnp
from jax import lax
from jax.experimental import pallas as pl
from jax.experimental.pallas import tpu as pltpu
from jax.sharding import PartitionSpec as P

HEAD_DIM = 256
SOFTCAP = 50.0
SCALE = 1.0 / math.sqrt(HEAD_DIM)
AXES = ("ctx", "head")
Z, Y = 8, 8
PIECE = 32
BLOCK = 256
BLOCKS = 64
SPAN = 640


def device_at(y, xlo, z, xhi, core):
    return (((y * 2 + xlo) * Z + z) * 2 + xhi) * 2 + core


def worker(block, kv_head):
    y, rest = divmod(block, 8)
    x, core = divmod(rest, 2)
    xhi, xlo = divmod(x, 2)
    return device_at(y, xlo, kv_head, xhi, core)


def spread_perm(turn):
    pairs = []
    for y in range(Y):
        for xlo in range(2):
            for z in range(Z):
                for part in range(4):
                    piece = (z % 2) * 4 + part
                    block = y * 8 + xlo * 4 + z // 2
                    pairs.append(
                        (
                            device_at(y, xlo, z, part // 2, part % 2),
                            worker(block, (piece + turn) % 8),
                        )
                    )
    return pairs


def window_perm(steps):
    return [
        (worker(block, kv_head), worker((block + steps) % BLOCKS, kv_head))
        for block in range(BLOCKS)
        for kv_head in range(8)
    ]


def backward(pairs):
    return [(target, source) for source, target in pairs]


def vmem_call(kernel, out_shape, args, scratch=(), flops=0, transcendentals=0):
    spec = pl.BlockSpec(memory_space=pltpu.VMEM)
    moved = sum(a.size * a.dtype.itemsize for a in jax.tree.leaves((args, out_shape)))
    return pl.pallas_call(
        kernel,
        out_shape=out_shape,
        in_specs=[pl.BlockSpec(memory_space=pltpu.SMEM)] + [spec] * (len(args) - 1),
        out_specs=jax.tree.map(lambda _: spec, out_shape),
        scratch_shapes=list(scratch),
        cost_estimate=pl.CostEstimate(
            flops=flops, bytes_accessed=moved, transcendentals=transcendentals
        ),
    )(*args)


def pack_kernel(place, q_ref, k_ref, v_ref, g_ref, *outs):
    for turn in range(8):
        kv_head = (place[0] + turn) & 7
        wide = pl.ds(pl.multiple_of(kv_head * 512, 512), 512)
        narrow = pl.ds(pl.multiple_of(kv_head * 256, 256), 256)
        outs[turn][:, 0:512] = q_ref[:, wide]
        outs[turn][:, 512:1024] = g_ref[:, wide]
        outs[turn][:, 1024:1280] = k_ref[:, narrow]
        outs[turn][:, 1280:1536] = v_ref[:, narrow]


def piece_of(place, turn):
    return (place[1] - turn + 8) & 7


def keys_kernel(place, *refs):
    out = refs[8]
    for turn in range(8):
        row = pl.multiple_of(piece_of(place, turn) * PIECE, PIECE)
        out[pl.ds(row, PIECE), :] = refs[turn][:, 1024:1536]


def dot(left, right, contract):
    return lax.dot_general(
        left, right, (contract, ((), ())), preferred_element_type=jnp.float32
    )


def attention_kernel(place, *refs):
    pieces, (kv0, kv1, kv2) = refs[:8], refs[8:11]
    query_grad, own, near, far = refs[11:15]
    qs, gs, keys, values, scores, dweights, low_w, low_s, key_acc, value_acc, slopes = refs[15:]
    for turn in range(8):
        piece = piece_of(place, turn)
        row = pl.multiple_of((piece // 4) * 256 + (piece % 4) * PIECE, PIECE)
        for n in range(2):
            rows = pl.ds(row + n * 128, PIECE)
            qs[rows, :] = pieces[turn][:, n * 256 : n * 256 + 256]
            gs[rows, :] = pieces[turn][:, 512 + n * 256 : 768 + n * 256]
    for idx, kv in enumerate((kv2, kv1, kv0)):
        keys[idx * 256 : idx * 256 + 256, :] = kv[:, 0:256]
        values[idx * 256 : idx * 256 + 256, :] = kv[:, 256:512]
    block = place[2]
    for i in range(2):
        low = i * 128
        queries = qs[i * 256 : i * 256 + 256, :]
        grads = gs[i * 256 : i * 256 + 256, :]
        k_win = keys[low : low + SPAN, :]
        v_win = values[low : low + SPAN, :]
        scores[...] = dot(k_win, queries, ((1,), (1,)))
        dweights[...] = dot(v_win, grads, ((1,), (1,)))
        first = 512 - block * BLOCK - low
        token = lax.broadcasted_iota(jnp.int32, (16, 256), 1) & 127
        start = jnp.maximum(token + 1, first)
        stop = token + 512
        key_row = lax.broadcasted_iota(jnp.int32, (16, 256), 0)

        def sums(step, carry):
            total, delta = carry
            rows = pl.ds(pl.multiple_of(step * 16, 16), 16)
            bent = jnp.tanh(scores[rows, :] * (SCALE / SOFTCAP))
            row = key_row + step * 16
            weight = jnp.where((row >= start) & (row <= stop), jnp.exp(SOFTCAP * bent), 0.0)
            scores[rows, :] = weight
            total = total + weight
            dw = dweights[rows, :]
            delta = delta + weight * dw
            slope = weight * (SCALE - SCALE * (bent * bent))
            slopes[rows, :] = slope
            return total, delta

        zero = jnp.zeros((16, 256), jnp.float32)
        total, delta = lax.fori_loop(0, SPAN // 16, sums, (zero, zero), unroll=4)
        inverse = 1.0 / jnp.sum(total, axis=0, keepdims=True)
        delta = jnp.sum(delta, axis=0, keepdims=True) * inverse
        inverse = jnp.broadcast_to(inverse, (16, 256))
        delta = jnp.broadcast_to(delta, (16, 256))

        def finish(step, carry):
            rows = pl.ds(pl.multiple_of(step * 16, 16), 16)
            low_w[rows, :] = (scores[rows, :] * inverse).astype(jnp.bfloat16)
            low_s[rows, :] = (
                slopes[rows, :] * inverse * (dweights[rows, :] - delta)
            ).astype(jnp.bfloat16)
            return carry

        lax.fori_loop(0, SPAN // 16, finish, 0, unroll=4)
        rows_grad = dot(low_s[...], k_win, ((0,), (0,))).astype(jnp.bfloat16)
        for n in range(2):
            query_grad[low : low + 128, n * 256 : n * 256 + 256] = rows_grad[
                n * 128 : n * 128 + 128, :
            ]
        key_part = dot(low_s[...], queries, ((1,), (0,)))
        value_part = dot(low_w[...], grads, ((1,), (0,)))
        if i == 0:
            key_acc[0:SPAN, :] = key_part
            value_acc[0:SPAN, :] = value_part
        else:
            key_acc[128:SPAN, :] += key_part[0:512, :]
            value_acc[128:SPAN, :] += value_part[0:512, :]
            key_acc[SPAN:768, :] = key_part[512:SPAN, :]
            value_acc[SPAN:768, :] = value_part[512:SPAN, :]
    for idx, out in enumerate((far, near, own)):
        out[:, 0:256] = key_acc[idx * 256 : idx * 256 + 256, :].astype(out.dtype)
        out[:, 256:512] = value_acc[idx * 256 : idx * 256 + 256, :].astype(out.dtype)


def exit_kernel(place, query_grad, own, near, far, *outs):
    for turn in range(8):
        rows = pl.ds(pl.multiple_of(piece_of(place, turn) * PIECE, PIECE), PIECE)
        outs[turn][:, 0:512] = query_grad[rows, :]
        total = own[rows, :] + near[rows, :].astype(jnp.float32) + far[rows, :].astype(jnp.float32)
        outs[turn][:, 512:1024] = total.astype(jnp.bfloat16)


def unpack_kernel(place, *refs):
    pieces, (q_ref, k_ref, v_ref) = refs[:8], refs[8:]
    for turn in range(8):
        kv_head = (place[0] + turn) & 7
        wide = pl.ds(pl.multiple_of(kv_head * 512, 512), 512)
        narrow = pl.ds(pl.multiple_of(kv_head * 256, 256), 256)
        q_ref[:, wide] = pieces[turn][:, 0:512]
        k_ref[:, narrow] = pieces[turn][:, 512:768]
        v_ref[:, narrow] = pieces[turn][:, 768:1024]


def shape(rows, cols, dtype=jnp.bfloat16):
    return jax.ShapeDtypeStruct((rows, cols), dtype)


def shards(query_proj, key_proj, value_proj, out_grad):
    ctx, head = lax.axis_index("ctx"), lax.axis_index("head")
    z, xlo, y = ctx % Z, (ctx // Z) % 2, ctx // (2 * Z)
    xhi, core = head // 2, head % 2
    block = y * 8 + (xhi * 2 + xlo) * 2 + core
    place = jnp.stack([(z % 2) * 4 + head, z, block]).astype(jnp.int32)
    packed = vmem_call(
        pack_kernel, [shape(32, 1536)] * 8, (place, query_proj, key_proj, value_proj, out_grad)
    )
    pieces = [lax.ppermute(packed[turn], AXES, spread_perm(turn)) for turn in range(8)]
    kv = vmem_call(keys_kernel, shape(BLOCK, 512), (place, *pieces))
    near_kv = lax.ppermute(kv, AXES, window_perm(1))
    far_kv = lax.ppermute(kv, AXES, window_perm(2))
    query_grad, own, near, far = vmem_call(
        attention_kernel,
        (shape(BLOCK, 512), shape(BLOCK, 512, jnp.float32), shape(BLOCK, 512), shape(BLOCK, 512)),
        (place, *pieces, kv, near_kv, far_kv),
        scratch=[
            pltpu.VMEM((512, 256), jnp.bfloat16),
            pltpu.VMEM((512, 256), jnp.bfloat16),
            pltpu.VMEM((768, 256), jnp.bfloat16),
            pltpu.VMEM((768, 256), jnp.bfloat16),
            pltpu.VMEM((SPAN, 256), jnp.float32),
            pltpu.VMEM((SPAN, 256), jnp.float32),
            pltpu.VMEM((SPAN, 256), jnp.bfloat16),
            pltpu.VMEM((SPAN, 256), jnp.bfloat16),
            pltpu.VMEM((768, 256), jnp.float32),
            pltpu.VMEM((768, 256), jnp.float32),
            pltpu.VMEM((SPAN, 256), jnp.float32),
        ],
        flops=2 * 5 * 2 * 256 * 640 * 256,
        transcendentals=2 * 2 * 256 * 640,
    )
    near = lax.ppermute(near, AXES, backward(window_perm(1)))
    far = lax.ppermute(far, AXES, backward(window_perm(2)))
    packed = vmem_call(
        exit_kernel, [shape(32, 1024)] * 8, (place, query_grad, own, near, far)
    )
    pieces = [lax.ppermute(packed[turn], AXES, backward(spread_perm(turn))) for turn in range(8)]
    return vmem_call(
        unpack_kernel, (shape(32, 4096), shape(32, 2048), shape(32, 2048)), (place, *pieces)
    )


def solution(mesh):
    spec = P(AXES, None)
    return jax.shard_map(
        shards, mesh=mesh, in_specs=(spec,) * 4, out_specs=(spec,) * 3, check_vma=False
    )
```

```python
import math

import jax
import jax.numpy as jnp
from jax import lax
from jax.experimental import pallas as pl
from jax.experimental.pallas import tpu as pltpu
from jax.sharding import Mesh, PartitionSpec as P

HEAD_DIM = 256
SOFTCAP = 50.0
SCALE = 1.0 / math.sqrt(HEAD_DIM)
NAMES = ("y", "xlo", "z", "xhi", "core")
SIZES = (8, 2, 8, 2, 2)
LINES = 16
PIECE = 32
PAIR = 672
SPAN = 1536


def line_perm(steps):
    return [(line, (line + steps) % LINES) for line in range(LINES)]


CORE_PERM = [(0, 1), (1, 0)]


def vmem_call(kernel, out_shape, args, scratch=(), flops=0, transcendentals=0, places=0):
    spec = pl.BlockSpec(memory_space=pltpu.VMEM)
    moved = sum(a.size * a.dtype.itemsize for a in jax.tree.leaves((args, out_shape)))
    return pl.pallas_call(
        kernel,
        out_shape=out_shape,
        in_specs=[pl.BlockSpec(memory_space=pltpu.SMEM)] * places + [spec] * (len(args) - places),
        out_specs=jax.tree.map(lambda _: spec, out_shape),
        scratch_shapes=list(scratch),
        cost_estimate=pl.CostEstimate(
            flops=flops, bytes_accessed=moved, transcendentals=transcendentals
        ),
    )(*args)


def pack_kv_kernel(k_ref, v_ref, out):
    for head in range(8):
        cols = slice(head * 256, head * 256 + 256)
        for xhi in range(2):
            out[head * 2 + xhi, :, 0:256] = k_ref[:, cols]
            out[head * 2 + xhi, :, 256:512] = v_ref[:, cols]


def pack_qg_kernel(q_ref, g_ref, out):
    for head in range(8):
        cols = slice(head * 512, head * 512 + 512)
        out[head, :, 0:512] = q_ref[:, cols]
        out[head, :, 512:1024] = g_ref[:, cols]


def dot(left, right, contract):
    return lax.dot_general(
        left, right, (contract, ((), ())), preferred_element_type=jnp.float32
    )


def piece_rows(place, other, base, idx):
    core = place[1]
    if other:
        core = 1 - core
    start = base + (idx // 2) * 128 + (idx % 2) * 64 + core * PIECE
    return pl.ds(pl.multiple_of(start, PIECE), PIECE)


def attention_kernel(place, qg, own, other, prev_own, prev_other, *refs):
    query_grad, line_mine, prev_mine, line_theirs, prev_theirs = refs[:5]
    qs, gs, keys, values, scores, dweights, slopes, low_w, low_s, key_acc, value_acc = refs[5:]
    for z in range(8):
        for n in range(2):
            rows = slice(z * 64 + n * PIECE, z * 64 + n * PIECE + PIECE)
            qs[rows, :] = qg[z, :, n * 256 : n * 256 + 256]
            gs[rows, :] = qg[z, :, 512 + n * 256 : 768 + n * 256]
    for source, is_other, base, count in (
        (own, False, 512, 16),
        (other, True, 512, 16),
        (prev_own, False, 0, 8),
        (prev_other, True, 0, 8),
    ):
        for idx in range(count):
            rows = piece_rows(place, is_other, base, idx)
            keys[rows, :] = source[idx, :, 0:256]
            values[rows, :] = source[idx, :, 256:512]
    key_acc[...] = jnp.zeros_like(key_acc)
    value_acc[...] = jnp.zeros_like(value_acc)
    offset = place[0] * PIECE
    column = lax.broadcasted_iota(jnp.int32, (16, 128), 1)
    token = (column // 64) * 128 + (column & 31)
    stop = token + 512
    key_row = lax.broadcasted_iota(jnp.int32, (16, 128), 0)
    for pair in range(4):
        low = 256 * pair + offset
        window = pl.ds(pl.multiple_of(low, PIECE), PAIR)
        queries = qs[pair * 128 : pair * 128 + 128, :]
        grads = gs[pair * 128 : pair * 128 + 128, :]
        scores[...] = dot(keys[window, :], queries, ((1,), (1,)))
        dweights[...] = dot(values[window, :], grads, ((1,), (1,)))
        start = jnp.maximum(token + 1, jnp.where(place[2] == 0, 512 - low, 0))

        def sums(step, carry):
            total, delta = carry
            rows = pl.ds(pl.multiple_of(step * 16, 16), 16)
            bent = jnp.tanh(scores[rows, :] * (SCALE / SOFTCAP))
            row = key_row + step * 16
            weight = jnp.where((row >= start) & (row <= stop), jnp.exp(SOFTCAP * bent), 0.0)
            scores[rows, :] = weight
            total = total + weight
            delta = delta + weight * dweights[rows, :]
            slopes[rows, :] = weight * (SCALE - SCALE * (bent * bent))
            return total, delta

        zero = jnp.zeros((16, 128), jnp.float32)
        total, delta = lax.fori_loop(0, PAIR // 16, sums, (zero, zero), unroll=6)
        inverse = 1.0 / jnp.sum(total, axis=0, keepdims=True)
        delta = jnp.sum(delta, axis=0, keepdims=True) * inverse
        inverse = jnp.broadcast_to(inverse, (16, 128))
        delta = jnp.broadcast_to(delta, (16, 128))

        def finish(step, carry):
            rows = pl.ds(pl.multiple_of(step * 16, 16), 16)
            low_w[rows, :] = (scores[rows, :] * inverse).astype(jnp.bfloat16)
            low_s[rows, :] = (slopes[rows, :] * inverse * (dweights[rows, :] - delta)).astype(
                jnp.bfloat16
            )
            return carry

        lax.fori_loop(0, PAIR // 16, finish, 0, unroll=6)
        rows_grad = dot(low_s[...], keys[window, :], ((0,), (0,))).astype(jnp.bfloat16)
        for z in range(2):
            for n in range(2):
                first = z * 64 + n * PIECE
                query_grad[pair * 2 + z, :, n * 256 : n * 256 + 256] = rows_grad[
                    first : first + PIECE, :
                ]
        key_acc[window, :] += dot(low_s[...], queries, ((1,), (0,)))
        value_acc[window, :] += dot(low_w[...], grads, ((1,), (0,)))
    for target, is_other, base, count in (
        (prev_theirs, True, 0, 8),
        (line_theirs, True, 512, 16),
        (prev_mine, False, 0, 8),
        (line_mine, False, 512, 16),
    ):
        for idx in range(count):
            rows = piece_rows(place, is_other, base, idx)
            target[idx, :, 0:256] = key_acc[rows, :].astype(target.dtype)
            target[idx, :, 256:512] = value_acc[rows, :].astype(target.dtype)


def sum_prev_kernel(mine, received, out):
    out[...] = (mine[...] + received[...].astype(jnp.float32)).astype(jnp.bfloat16)


def sum_line_kernel(mine, received, later, out):
    for idx in range(16):
        total = mine[idx] + received[idx].astype(jnp.float32)
        if idx >= 8:
            total = total + later[idx - 8].astype(jnp.float32)
        out[idx] = total.astype(jnp.bfloat16)


def unpack_q_kernel(pieces, q_ref):
    for head in range(8):
        q_ref[:, head * 512 : head * 512 + 512] = pieces[head]


def unpack_kv_kernel(pieces, k_ref, v_ref):
    for head in range(8):
        total = pieces[head * 2].astype(jnp.float32) + pieces[head * 2 + 1].astype(jnp.float32)
        total = total.astype(jnp.bfloat16)
        k_ref[:, head * 256 : head * 256 + 256] = total[:, 0:256]
        v_ref[:, head * 256 : head * 256 + 256] = total[:, 256:512]


def struct(*dims, dtype=jnp.bfloat16):
    return jax.ShapeDtypeStruct(dims, dtype)


def exchange(value, axes):
    return lax.all_to_all(value, axes, split_axis=0, concat_axis=0, tiled=True)


def shards(query_proj, key_proj, value_proj, out_grad):
    y, xlo, xhi, core = (lax.axis_index(name) for name in ("y", "xlo", "xhi", "core"))
    place = jnp.stack([xhi * 2 + core, core, y * 2 + xlo]).astype(jnp.int32)
    kv = exchange(vmem_call(pack_kv_kernel, struct(16, 32, 512), (key_proj, value_proj)), ("z", "xhi"))
    prev_kv = lax.ppermute(kv[8:16], ("y", "xlo"), line_perm(1))
    other_kv = lax.ppermute(kv, "core", CORE_PERM)
    qg = exchange(vmem_call(pack_qg_kernel, struct(8, 32, 1024), (query_proj, out_grad)), "z")
    prev_other = lax.ppermute(prev_kv, "core", CORE_PERM)
    f32, bf16 = jnp.float32, jnp.bfloat16
    query_grad, line_mine, prev_mine, line_theirs, prev_theirs = vmem_call(
        attention_kernel,
        (
            struct(8, 32, 512),
            struct(16, 32, 512, dtype=f32),
            struct(8, 32, 512, dtype=f32),
            struct(16, 32, 512),
            struct(8, 32, 512),
        ),
        (place, qg, kv, other_kv, prev_kv, prev_other),
        scratch=[
            pltpu.VMEM((512, 256), bf16),
            pltpu.VMEM((512, 256), bf16),
            pltpu.VMEM((SPAN, 256), bf16),
            pltpu.VMEM((SPAN, 256), bf16),
            pltpu.VMEM((PAIR, 128), f32),
            pltpu.VMEM((PAIR, 128), f32),
            pltpu.VMEM((PAIR, 128), f32),
            pltpu.VMEM((PAIR, 128), bf16),
            pltpu.VMEM((PAIR, 128), bf16),
            pltpu.VMEM((SPAN, 256), f32),
            pltpu.VMEM((SPAN, 256), f32),
        ],
        flops=2 * 5 * 4 * PAIR * 128 * 256,
        transcendentals=2 * 4 * PAIR * 128,
        places=1,
    )
    prev_received = lax.ppermute(prev_theirs, "core", CORE_PERM)
    line_received = lax.ppermute(line_theirs, "core", CORE_PERM)
    later = lax.ppermute(
        vmem_call(sum_prev_kernel, struct(8, 32, 512), (prev_mine, prev_received)),
        ("y", "xlo"),
        line_perm(-1),
    )
    query_out = exchange(query_grad, "z")
    kv_out = exchange(
        vmem_call(sum_line_kernel, struct(16, 32, 512), (line_mine, line_received, later)),
        ("z", "xhi"),
    )
    key_out, value_out = vmem_call(
        unpack_kv_kernel, (struct(32, 2048), struct(32, 2048)), (kv_out,)
    )
    return vmem_call(unpack_q_kernel, struct(32, 4096), (query_out,)), key_out, value_out


def solution(mesh):
    fine = Mesh(mesh.devices.reshape(SIZES), NAMES)
    spec = P(NAMES, None)
    return jax.shard_map(
        shards, mesh=fine, in_specs=(spec,) * 4, out_specs=(spec,) * 3, check_vma=False
    )
```

```python
import math

import jax
import jax.numpy as jnp
from jax import lax
from jax.experimental import pallas as pl
from jax.experimental.pallas import tpu as pltpu
from jax.sharding import Mesh, PartitionSpec as P

HEAD_DIM = 256
SOFTCAP = 50.0
SCALE = 1.0 / math.sqrt(HEAD_DIM)
NAMES = ("y", "xlo", "z", "xhi", "core")
SIZES = (8, 2, 8, 2, 2)
LINES = 16
PIECE = 32
PAIR = 672
SPAN = 1536


def line_perm(steps):
    return [(line, (line + steps) % LINES) for line in range(LINES)]


def cross_perm(steps):
    return [
        (line * 2 + xhi, (line + steps) % LINES * 2 + 1 - xhi)
        for line in range(LINES)
        for xhi in range(2)
    ]


SWAP = [(0, 1), (1, 0)]


def vmem_call(kernel, out_shape, args, scratch=(), flops=0, transcendentals=0, places=0):
    spec = pl.BlockSpec(memory_space=pltpu.VMEM)
    moved = sum(a.size * a.dtype.itemsize for a in jax.tree.leaves((args, out_shape)))
    return pl.pallas_call(
        kernel,
        out_shape=out_shape,
        in_specs=[pl.BlockSpec(memory_space=pltpu.SMEM)] * places + [spec] * (len(args) - places),
        out_specs=jax.tree.map(lambda _: spec, out_shape),
        scratch_shapes=list(scratch),
        compiler_params=pltpu.CompilerParams(
            vmem_limit_bytes=moved + moved // 8 + ((10 if scratch else 1) << 20)
        ),
        cost_estimate=pl.CostEstimate(
            flops=flops, bytes_accessed=moved, transcendentals=transcendentals
        ),
    )(*args)


def pack_kv_kernel(k_ref, v_ref, out):
    for head in range(8):
        cols = slice(head * 256, head * 256 + 256)
        out[head, :, 0:256] = k_ref[:, cols]
        out[head, :, 256:512] = v_ref[:, cols]


def pack_qg_kernel(q_ref, g_ref, out):
    for head in range(8):
        cols = slice(head * 512, head * 512 + 512)
        out[head, :, 0:512] = q_ref[:, cols]
        out[head, :, 512:1024] = g_ref[:, cols]


def dot(left, right, contract):
    return lax.dot_general(
        left, right, (contract, ((), ())), preferred_element_type=jnp.float32
    )


def piece_rows(place, base, chunk, other_x, other_c):
    xhi = 1 - place[0] if other_x else place[0]
    core = 1 - place[1] if other_c else place[1]
    return pl.ds(pl.multiple_of(base + chunk * 128 + xhi * 64 + core * PIECE, PIECE), PIECE)


def reach_rows(place, idx, other_c):
    if idx < 8:
        return piece_rows(place, 512, idx, True, other_c)
    return piece_rows(place, 0, idx % 4, idx >= 12, other_c)


def attention_kernel(place, qg, own, partner, across, before, before_across, reach, *refs):
    query_grad, mine, mine_reach, theirs, theirs_reach = refs[:5]
    qs, gs, keys, values, scores, dweights, slopes, low_w, low_s, key_acc, value_acc = refs[5:]

    def put(rows, piece):
        keys[rows, :] = piece[:, 0:256]
        values[rows, :] = piece[:, 256:512]

    for z in range(8):
        put(piece_rows(place, 512, z, False, False), own[z])
        put(piece_rows(place, 512, z, False, True), partner[z])
        put(piece_rows(place, 512, z, True, False), across[z])
    for z in range(4):
        put(piece_rows(place, 0, z, False, False), before[z])
        put(piece_rows(place, 0, z, True, False), before_across[z])
    for idx in range(16):
        put(reach_rows(place, idx, True), reach[idx])
    for z in range(8):
        for n in range(2):
            rows = slice(z * 64 + n * PIECE, z * 64 + n * PIECE + PIECE)
            qs[rows, :] = qg[z, :, n * 256 : n * 256 + 256]
            gs[rows, :] = qg[z, :, 512 + n * 256 : 768 + n * 256]
    key_acc[...] = jnp.zeros_like(key_acc)
    value_acc[...] = jnp.zeros_like(value_acc)
    offset = place[0] * 64 + place[1] * PIECE
    column = lax.broadcasted_iota(jnp.int32, (16, 128), 1)
    token = (column // 64) * 128 + (column & 31)
    stop = token + 512
    key_row = lax.broadcasted_iota(jnp.int32, (16, 128), 0)
    for pair in range(4):
        low = 256 * pair + offset
        window = pl.ds(pl.multiple_of(low, PIECE), PAIR)
        queries = qs[pair * 128 : pair * 128 + 128, :]
        grads = gs[pair * 128 : pair * 128 + 128, :]
        scores[...] = dot(keys[window, :], queries, ((1,), (1,)))
        dweights[...] = dot(values[window, :], grads, ((1,), (1,)))
        start = jnp.maximum(token + 1, jnp.where(place[2] == 0, 512 - low, 0))

        def sums(step, carry):
            total, delta = carry
            rows = pl.ds(pl.multiple_of(step * 16, 16), 16)
            bent = jnp.tanh(scores[rows, :] * (SCALE / SOFTCAP))
            row = key_row + step * 16
            weight = jnp.where((row >= start) & (row <= stop), jnp.exp(SOFTCAP * bent), 0.0)
            scores[rows, :] = weight
            total = total + weight
            delta = delta + weight * dweights[rows, :]
            slopes[rows, :] = weight * (SCALE - SCALE * (bent * bent))
            return total, delta

        zero = jnp.zeros((16, 128), jnp.float32)
        total, delta = lax.fori_loop(0, PAIR // 16, sums, (zero, zero), unroll=6)
        inverse = 1.0 / jnp.sum(total, axis=0, keepdims=True)
        delta = jnp.sum(delta, axis=0, keepdims=True) * inverse
        inverse = jnp.broadcast_to(inverse, (16, 128))
        delta = jnp.broadcast_to(delta, (16, 128))

        def finish(step, carry):
            rows = pl.ds(pl.multiple_of(step * 16, 16), 16)
            low_w[rows, :] = (scores[rows, :] * inverse).astype(jnp.bfloat16)
            low_s[rows, :] = (slopes[rows, :] * inverse * (dweights[rows, :] - delta)).astype(
                jnp.bfloat16
            )
            return carry

        lax.fori_loop(0, PAIR // 16, finish, 0, unroll=6)
        rows_grad = dot(low_s[...], keys[window, :], ((0,), (0,))).astype(jnp.bfloat16)
        for z in range(2):
            for n in range(2):
                first = z * 64 + n * PIECE
                query_grad[pair * 2 + z, :, n * 256 : n * 256 + 256] = rows_grad[
                    first : first + PIECE, :
                ]
        key_acc[window, :] += dot(low_s[...], queries, ((1,), (0,)))
        value_acc[window, :] += dot(low_w[...], grads, ((1,), (0,)))

    def take(target, idx, rows):
        target[idx, :, 0:256] = key_acc[rows, :].astype(target.dtype)
        target[idx, :, 256:512] = value_acc[rows, :].astype(target.dtype)

    for idx in range(16):
        take(theirs_reach, idx, reach_rows(place, idx, True))
        take(mine_reach, idx, reach_rows(place, idx, False))
    for z in range(8):
        take(theirs, z, piece_rows(place, 512, z, False, True))
        take(mine, z, piece_rows(place, 512, z, False, False))


def sum_reach_kernel(mine, received, across, before, before_across):
    for idx in range(16):
        total = (mine[idx] + received[idx].astype(jnp.float32)).astype(jnp.bfloat16)
        if idx < 8:
            across[idx] = total
        elif idx < 12:
            before[idx - 8] = total
        else:
            before_across[idx - 12] = total


def sum_own_kernel(mine, partner, across, after, after_across, out):
    for z in range(8):
        total = mine[z] + partner[z].astype(jnp.float32) + across[z].astype(jnp.float32)
        if z >= 4:
            total = total + after[z - 4].astype(jnp.float32)
            total = total + after_across[z - 4].astype(jnp.float32)
        out[z] = total.astype(jnp.bfloat16)


def unpack_q_kernel(pieces, q_ref):
    for head in range(8):
        q_ref[:, head * 512 : head * 512 + 512] = pieces[head]


def unpack_kv_kernel(pieces, k_ref, v_ref):
    for head in range(8):
        k_ref[:, head * 256 : head * 256 + 256] = pieces[head, :, 0:256]
        v_ref[:, head * 256 : head * 256 + 256] = pieces[head, :, 256:512]


def struct(*dims, dtype=jnp.bfloat16):
    return jax.ShapeDtypeStruct(dims, dtype)


def exchange(value):
    return lax.all_to_all(value, "z", split_axis=0, concat_axis=0, tiled=True)


LINE, CROSS = ("y", "xlo"), ("y", "xlo", "xhi")


def shards(query_proj, key_proj, value_proj, out_grad):
    y, xlo, xhi, core = (lax.axis_index(name) for name in ("y", "xlo", "xhi", "core"))
    place = jnp.stack([xhi, core, y * 2 + xlo]).astype(jnp.int32)
    own = exchange(vmem_call(pack_kv_kernel, struct(8, 32, 512), (key_proj, value_proj)))
    across = lax.ppermute(own, "xhi", SWAP)
    before = lax.ppermute(own[4:8], LINE, line_perm(1))
    before_across = lax.ppermute(own[4:8], CROSS, cross_perm(1))
    partner = lax.ppermute(own, "core", SWAP)
    qg = exchange(vmem_call(pack_qg_kernel, struct(8, 32, 1024), (query_proj, out_grad)))
    reach = lax.ppermute(
        jnp.concatenate([across, before, before_across], axis=0), "core", SWAP
    )
    f32, bf16 = jnp.float32, jnp.bfloat16
    query_grad, mine, mine_reach, theirs, theirs_reach = vmem_call(
        attention_kernel,
        (
            struct(8, 32, 512),
            struct(8, 32, 512, dtype=f32),
            struct(16, 32, 512, dtype=f32),
            struct(8, 32, 512),
            struct(16, 32, 512),
        ),
        (place, qg, own, partner, across, before, before_across, reach),
        scratch=[
            pltpu.VMEM((512, 256), bf16),
            pltpu.VMEM((512, 256), bf16),
            pltpu.VMEM((SPAN, 256), bf16),
            pltpu.VMEM((SPAN, 256), bf16),
            pltpu.VMEM((PAIR, 128), f32),
            pltpu.VMEM((PAIR, 128), f32),
            pltpu.VMEM((PAIR, 128), f32),
            pltpu.VMEM((PAIR, 128), bf16),
            pltpu.VMEM((PAIR, 128), bf16),
            pltpu.VMEM((SPAN, 256), f32),
            pltpu.VMEM((SPAN, 256), f32),
        ],
        flops=2 * 5 * 4 * PAIR * 128 * 256,
        transcendentals=2 * 4 * PAIR * 128,
        places=1,
    )
    reach_received = lax.ppermute(theirs_reach, "core", SWAP)
    received = lax.ppermute(theirs, "core", SWAP)
    across, before, before_across = vmem_call(
        sum_reach_kernel,
        (struct(8, 32, 512), struct(4, 32, 512), struct(4, 32, 512)),
        (mine_reach, reach_received),
    )
    across = lax.ppermute(across, "xhi", SWAP)
    after = lax.ppermute(before, LINE, line_perm(-1))
    after_across = lax.ppermute(before_across, CROSS, cross_perm(-1))
    query_out = exchange(query_grad)
    kv_out = exchange(
        vmem_call(
            sum_own_kernel,
            struct(8, 32, 512),
            (mine, received, across, after, after_across),
        )
    )
    key_out, value_out = vmem_call(
        unpack_kv_kernel, (struct(32, 2048), struct(32, 2048)), (kv_out,)
    )
    return vmem_call(unpack_q_kernel, struct(32, 4096), (query_out,)), key_out, value_out


def solution(mesh):
    fine = Mesh(mesh.devices.reshape(SIZES), NAMES)
    spec = P(NAMES, None)
    return jax.shard_map(
        shards, mesh=fine, in_specs=(spec,) * 4, out_specs=(spec,) * 3, check_vma=False
    )
```

```python
import functools
import math

import jax
import jax.numpy as jnp
from jax import lax
from jax.experimental import pallas as pl
from jax.experimental.pallas import tpu as pltpu
from jax.sharding import Mesh, PartitionSpec as P


HEAD_DIM = 256
SOFTCAP = 50.0
SCALE = 1.0 / math.sqrt(HEAD_DIM)
NAMES = ("y", "xlo", "z", "xhi", "core")
SIZES = (8, 2, 8, 2, 2)
LINES = 16
PIECE = 32
PAIR = 672
SPAN = 1536


def line_perm(steps):
    return [
        (line, line + steps) for line in range(max(0, -steps), min(LINES, LINES - steps))
    ]


def cross_perm(steps):
    return [
        (source * 2 + xhi, target * 2 + 1 - xhi)
        for source, target in line_perm(steps)
        for xhi in range(2)
    ]


SWAP = [(0, 1), (1, 0)]


def vmem_call(kernel, out_shape, args, scratch=(), flops=0, transcendentals=0, places=0, away=0, limit=16):
    spec = pl.BlockSpec(memory_space=pltpu.VMEM)
    remote = pl.BlockSpec(memory_space=pl.ANY)
    moved = sum(a.size * a.dtype.itemsize for a in jax.tree.leaves((args, out_shape)))
    return pl.pallas_call(
        kernel,
        out_shape=out_shape,
        in_specs=[pl.BlockSpec(memory_space=pltpu.SMEM)] * places
        + [remote] * away
        + [spec] * (len(args) - places - away),
        out_specs=jax.tree.map(lambda _: spec, out_shape),
        scratch_shapes=list(scratch),
        compiler_params=pltpu.CompilerParams(
            vmem_limit_bytes=limit << 20
        ),
        cost_estimate=pl.CostEstimate(
            flops=flops, bytes_accessed=moved, transcendentals=transcendentals
        ),
    )(*args)


def pack_kernel(width, left, right, out, sems):
    copies = []
    for head in range(8):
        for side, source in enumerate((left, right)):
            copies.append(
                pltpu.make_async_copy(
                    source.at[:, head * width : head * width + width],
                    out.at[head, :, side * width : side * width + width],
                    sems.at[head * 2 + side],
                )
            )
    for copy in copies:
        copy.start()
    for copy in copies:
        copy.wait()


def pack(left, right, limit=16):
    width = left.shape[1] // 8
    return vmem_call(
        functools.partial(pack_kernel, width),
        struct(8, 32, 2 * width),
        (left, right),
        scratch=[pltpu.SemaphoreType.DMA((16,))],
        away=2,
        limit=limit,
    )


def dot(left, right, contract):
    return lax.dot_general(
        left, right, (contract, ((), ())), preferred_element_type=jnp.float32
    )


def piece_rows(place, base, chunk, other_x, other_c):
    xhi = 1 - place[0] if other_x else place[0]
    core = 1 - place[1] if other_c else place[1]
    return pl.ds(pl.multiple_of(base + chunk * 128 + xhi * 64 + core * PIECE, PIECE), PIECE)


def reach_rows(place, idx, other_c):
    if idx < 8:
        return piece_rows(place, 512, idx, True, other_c)
    return piece_rows(place, 0, idx % 4, idx >= 12, other_c)


def attention_kernel(place, qg, own, partner, across, before, before_across, reach, *refs):
    query_grad, mine, mine_reach, theirs, theirs_reach = refs[:5]
    qs, gs, keys, values, scores, dweights, slopes, low_w, low_s, key_acc, value_acc = refs[5:]

    def put(rows, piece):
        keys[rows, :] = piece[:, 0:256]
        values[rows, :] = piece[:, 256:512]

    for z in range(8):
        put(piece_rows(place, 512, z, False, False), own[z])
        put(piece_rows(place, 512, z, False, True), partner[z])
        put(piece_rows(place, 512, z, True, False), across[z])
    for z in range(4):
        put(piece_rows(place, 0, z, False, False), before[z])
        put(piece_rows(place, 0, z, True, False), before_across[z])
    for idx in range(16):
        put(reach_rows(place, idx, True), reach[idx])
    for z in range(8):
        for n in range(2):
            rows = slice(z * 64 + n * PIECE, z * 64 + n * PIECE + PIECE)
            qs[rows, :] = qg[z, :, n * 256 : n * 256 + 256]
            gs[rows, :] = qg[z, :, 512 + n * 256 : 768 + n * 256]
    key_acc[...] = jnp.zeros_like(key_acc)
    value_acc[...] = jnp.zeros_like(value_acc)
    offset = place[0] * 64 + place[1] * PIECE
    column = lax.broadcasted_iota(jnp.int32, (16, 128), 1)
    token = (column // 64) * 128 + (column & 31)
    stop = token + 512
    key_row = lax.broadcasted_iota(jnp.int32, (16, 128), 0)
    for pair in range(4):
        low = 256 * pair + offset
        window = pl.ds(pl.multiple_of(low, PIECE), PAIR)
        queries = qs[pair * 128 : pair * 128 + 128, :]
        grads = gs[pair * 128 : pair * 128 + 128, :]
        scores[...] = dot(keys[window, :], queries, ((1,), (1,)))
        dweights[...] = dot(values[window, :], grads, ((1,), (1,)))
        start = jnp.maximum(token + 1, jnp.where(place[2] == 0, 512 - low, 0))

        def sums(step, carry):
            total, delta = carry
            rows = pl.ds(pl.multiple_of(step * 16, 16), 16)
            bent = jnp.tanh(scores[rows, :] * (SCALE / SOFTCAP))
            row = key_row + step * 16
            weight = jnp.where((row >= start) & (row <= stop), jnp.exp(SOFTCAP * bent), 0.0)
            scores[rows, :] = weight
            total = total + weight
            delta = delta + weight * dweights[rows, :]
            slopes[rows, :] = weight * (SCALE - SCALE * (bent * bent))
            return total, delta

        zero = jnp.zeros((16, 128), jnp.float32)
        total, delta = lax.fori_loop(0, PAIR // 16, sums, (zero, zero), unroll=21)
        inverse = 1.0 / jnp.sum(total, axis=0, keepdims=True)
        delta = jnp.sum(delta, axis=0, keepdims=True) * inverse
        inverse = jnp.broadcast_to(inverse, (16, 128))
        delta = jnp.broadcast_to(delta, (16, 128))

        def finish(step, carry):
            rows = pl.ds(pl.multiple_of(step * 16, 16), 16)
            low_w[rows, :] = (scores[rows, :] * inverse).astype(jnp.bfloat16)
            low_s[rows, :] = (slopes[rows, :] * inverse * (dweights[rows, :] - delta)).astype(
                jnp.bfloat16
            )
            return carry

        lax.fori_loop(0, PAIR // 16, finish, 0, unroll=21)
        rows_grad = dot(low_s[...], keys[window, :], ((0,), (0,))).astype(jnp.bfloat16)
        for z in range(2):
            for n in range(2):
                first = z * 64 + n * PIECE
                query_grad[pair * 2 + z, :, n * 256 : n * 256 + 256] = rows_grad[
                    first : first + PIECE, :
                ]
        key_acc[window, :] += dot(low_s[...], queries, ((1,), (0,)))
        value_acc[window, :] += dot(low_w[...], grads, ((1,), (0,)))

    def take(target, idx, rows):
        target[idx, :, 0:256] = key_acc[rows, :].astype(target.dtype)
        target[idx, :, 256:512] = value_acc[rows, :].astype(target.dtype)

    for idx in range(16):
        take(theirs_reach, idx, reach_rows(place, idx, True))
        take(mine_reach, idx, reach_rows(place, idx, False))
    for z in range(8):
        take(theirs, z, piece_rows(place, 512, z, False, True))
        take(mine, z, piece_rows(place, 512, z, False, False))


def sum_reach_kernel(mine, received, across, before, before_across):
    for idx in range(16):
        total = (mine[idx] + received[idx].astype(jnp.float32)).astype(jnp.bfloat16)
        if idx < 8:
            across[idx] = total
        elif idx < 12:
            before[idx - 8] = total
        else:
            before_across[idx - 12] = total


def sum_own_kernel(mine, partner, across, after, after_across, out):
    for z in range(8):
        total = mine[z] + partner[z].astype(jnp.float32) + across[z].astype(jnp.float32)
        if z >= 4:
            total = total + after[z - 4].astype(jnp.float32)
            total = total + after_across[z - 4].astype(jnp.float32)
        out[z] = total.astype(jnp.bfloat16)


def unpack_q_kernel(pieces, q_ref):
    for head in range(8):
        q_ref[:, head * 512 : head * 512 + 512] = pieces[head]


def unpack_kv_kernel(pieces, k_ref, v_ref):
    for head in range(8):
        k_ref[:, head * 256 : head * 256 + 256] = pieces[head, :, 0:256]
        v_ref[:, head * 256 : head * 256 + 256] = pieces[head, :, 256:512]


def struct(*dims, dtype=jnp.bfloat16):
    return jax.ShapeDtypeStruct(dims, dtype)


def exchange(value):
    return lax.all_to_all(value, "z", split_axis=0, concat_axis=0, tiled=True)


LINE, CROSS = ("y", "xlo"), ("y", "xlo", "xhi")


def shards(query_proj, key_proj, value_proj, out_grad):
    y, xlo, xhi, core = (lax.axis_index(name) for name in ("y", "xlo", "xhi", "core"))
    place = jnp.stack([xhi, core, y * 2 + xlo]).astype(jnp.int32)
    own = exchange(pack(key_proj, value_proj, limit=60))
    across = lax.ppermute(own, "xhi", SWAP)
    before = lax.ppermute(own[4:8], LINE, line_perm(1))
    before_across = lax.ppermute(own[4:8], CROSS, cross_perm(1))
    partner = lax.ppermute(own, "core", SWAP)
    qg = exchange(pack(query_proj, out_grad))
    reach = lax.ppermute(jnp.concatenate([across, before, before_across], axis=0), "core", SWAP)
    f32, bf16 = jnp.float32, jnp.bfloat16
    query_grad, mine, mine_reach, theirs, theirs_reach = vmem_call(
        attention_kernel,
        (
            struct(8, 32, 512),
            struct(8, 32, 512, dtype=f32),
            struct(16, 32, 512, dtype=f32),
            struct(8, 32, 512),
            struct(16, 32, 512),
        ),
        (place, qg, own, partner, across, before, before_across, reach),
        scratch=[
            pltpu.VMEM((512, 256), bf16),
            pltpu.VMEM((512, 256), bf16),
            pltpu.VMEM((SPAN, 256), bf16),
            pltpu.VMEM((SPAN, 256), bf16),
            pltpu.VMEM((PAIR, 128), f32),
            pltpu.VMEM((PAIR, 128), f32),
            pltpu.VMEM((PAIR, 128), f32),
            pltpu.VMEM((PAIR, 128), bf16),
            pltpu.VMEM((PAIR, 128), bf16),
            pltpu.VMEM((SPAN, 256), f32),
            pltpu.VMEM((SPAN, 256), f32),
        ],
        flops=2 * 5 * 4 * PAIR * 128 * 256,
        transcendentals=2 * 4 * PAIR * 128,
        places=1,
    )
    reach_received = lax.ppermute(theirs_reach, "core", SWAP)
    received = lax.ppermute(theirs, "core", SWAP)
    across, before, before_across = vmem_call(
        sum_reach_kernel,
        (struct(8, 32, 512), struct(4, 32, 512), struct(4, 32, 512)),
        (mine_reach, reach_received),
    )
    across = lax.ppermute(across, "xhi", SWAP)
    after = lax.ppermute(before, LINE, line_perm(-1))
    after_across = lax.ppermute(before_across, CROSS, cross_perm(-1))
    query_out = exchange(query_grad)
    kv_out = exchange(
        vmem_call(
            sum_own_kernel,
            struct(8, 32, 512),
            (mine, received, across, after, after_across),
        ),
    )
    key_out, value_out = vmem_call(
        unpack_kv_kernel, (struct(32, 2048), struct(32, 2048)), (kv_out,)
    )
    query_low = vmem_call(unpack_q_kernel, struct(32, 4096), (query_out,))
    return query_low, key_out, value_out


def solution(mesh):
    fine = Mesh(mesh.devices.reshape(SIZES), NAMES)
    spec = P(NAMES, None)
    return jax.shard_map(
        shards, mesh=fine, in_specs=(spec,) * 4, out_specs=(spec,) * 3, check_vma=False
    )
```

```python
import functools
import math

import jax
import jax.numpy as jnp
from jax import lax
from jax.experimental import pallas as pl
from jax.experimental.pallas import tpu as pltpu
from jax.sharding import Mesh, PartitionSpec as P


HEAD_DIM = 256
SOFTCAP = 50.0
SCALE = 1.0 / math.sqrt(HEAD_DIM)
NAMES = ("y", "xlo", "z", "xhi", "core")
SIZES = (8, 2, 8, 2, 2)
LINES = 16
PIECE = 32
PAIR = 672
SHARED = PAIR - 256
SPAN = 1536


def line_perm(steps):
    return [
        (line, line + steps) for line in range(max(0, -steps), min(LINES, LINES - steps))
    ]


def cross_perm(steps):
    return [
        (source * 2 + xhi, target * 2 + 1 - xhi)
        for source, target in line_perm(steps)
        for xhi in range(2)
    ]


SWAP = [(0, 1), (1, 0)]


def vmem_call(kernel, out_shape, args, scratch=(), flops=0, transcendentals=0, places=0, away=0, limit=16):
    spec = pl.BlockSpec(memory_space=pltpu.VMEM)
    remote = pl.BlockSpec(memory_space=pl.ANY)
    moved = sum(a.size * a.dtype.itemsize for a in jax.tree.leaves((args, out_shape)))
    return pl.pallas_call(
        kernel,
        out_shape=out_shape,
        in_specs=[pl.BlockSpec(memory_space=pltpu.SMEM)] * places
        + [remote] * away
        + [spec] * (len(args) - places - away),
        out_specs=jax.tree.map(lambda _: spec, out_shape),
        scratch_shapes=list(scratch),
        compiler_params=pltpu.CompilerParams(
            vmem_limit_bytes=limit << 20
        ),
        cost_estimate=pl.CostEstimate(
            flops=flops, bytes_accessed=moved, transcendentals=transcendentals
        ),
    )(*args)


def pack_kernel(width, left, right, out, sems):
    copies = []
    for head in range(8):
        for side, source in enumerate((left, right)):
            copies.append(
                pltpu.make_async_copy(
                    source.at[:, head * width : head * width + width],
                    out.at[head, :, side * width : side * width + width],
                    sems.at[head * 2 + side],
                )
            )
    for copy in copies:
        copy.start()
    for copy in copies:
        copy.wait()


def pack(left, right, limit=16):
    width = left.shape[1] // 8
    return vmem_call(
        functools.partial(pack_kernel, width),
        struct(8, 32, 2 * width),
        (left, right),
        scratch=[pltpu.SemaphoreType.DMA((16,))],
        away=2,
        limit=limit,
    )


def dot(left, right, contract):
    return lax.dot_general(
        left, right, (contract, ((), ())), preferred_element_type=jnp.float32
    )


def piece_rows(place, base, chunk, other_x, other_c):
    xhi = 1 - place[0] if other_x else place[0]
    core = 1 - place[1] if other_c else place[1]
    return pl.ds(pl.multiple_of(base + chunk * 128 + xhi * 64 + core * PIECE, PIECE), PIECE)


def reach_rows(place, idx, other_c):
    if idx < 8:
        return piece_rows(place, 512, idx, True, other_c)
    return piece_rows(place, 0, idx % 4, idx >= 12, other_c)


def attention_kernel(place, qg, own, partner, across, before, before_across, reach, *refs):
    query_grad, mine, mine_reach, theirs, theirs_reach = refs[:5]
    qs, gs, keys, values, scores, dweights, slopes, low_w, low_s, key_acc, value_acc = refs[5:]

    def put(rows, piece):
        keys[rows, :] = piece[:, 0:256]
        values[rows, :] = piece[:, 256:512]

    for z in range(8):
        put(piece_rows(place, 512, z, False, False), own[z])
        put(piece_rows(place, 512, z, False, True), partner[z])
        put(piece_rows(place, 512, z, True, False), across[z])
    for z in range(4):
        put(piece_rows(place, 0, z, False, False), before[z])
        put(piece_rows(place, 0, z, True, False), before_across[z])
    for idx in range(16):
        put(reach_rows(place, idx, True), reach[idx])
    for z in range(8):
        for n in range(2):
            rows = slice(z * 64 + n * PIECE, z * 64 + n * PIECE + PIECE)
            qs[rows, :] = qg[z, :, n * 256 : n * 256 + 256]
            gs[rows, :] = qg[z, :, 512 + n * 256 : 768 + n * 256]
    for acc in (key_acc, value_acc):
        acc[0:96, :] = jnp.zeros((96, 256), jnp.float32)
        acc[1440:SPAN, :] = jnp.zeros((96, 256), jnp.float32)
    offset = place[0] * 64 + place[1] * PIECE
    column = lax.broadcasted_iota(jnp.int32, (16, 128), 1)
    token = (column // 64) * 128 + (column & 31)
    stop = token + 512
    key_row = lax.broadcasted_iota(jnp.int32, (16, 128), 0)
    for pair in range(4):
        low = 256 * pair + offset
        window = pl.ds(pl.multiple_of(low, PIECE), PAIR)
        queries = qs[pair * 128 : pair * 128 + 128, :]
        grads = gs[pair * 128 : pair * 128 + 128, :]
        scores[...] = dot(keys[window, :], queries, ((1,), (1,)))
        dweights[...] = dot(values[window, :], grads, ((1,), (1,)))
        start = jnp.maximum(token + 1, jnp.where(place[2] == 0, 512 - low, 0))

        def sums(allowed, step, carry):
            total, delta = carry
            rows = pl.ds(pl.multiple_of(step * 16, 16), 16)
            bent = jnp.tanh(scores[rows, :] * (SCALE / SOFTCAP))
            weight = jnp.where(allowed(key_row + step * 16), jnp.exp(SOFTCAP * bent), 0.0)
            scores[rows, :] = weight
            total = total + weight
            delta = delta + weight * dweights[rows, :]
            slopes[rows, :] = weight * (SCALE - SCALE * (bent * bent))
            return total, delta

        zero = jnp.zeros((16, 128), jnp.float32)
        early = functools.partial(sums, lambda row: row >= start)
        late = functools.partial(sums, lambda row: row <= stop)
        total, delta = lax.fori_loop(0, 32, early, (zero, zero), unroll=16)
        total, delta = lax.fori_loop(32, PAIR // 16, late, (total, delta), unroll=10)
        inverse = 1.0 / jnp.sum(total, axis=0, keepdims=True)
        delta = jnp.sum(delta, axis=0, keepdims=True) * inverse
        inverse = jnp.broadcast_to(inverse, (16, 128))
        delta = jnp.broadcast_to(delta, (16, 128))

        def finish(step, carry):
            rows = pl.ds(pl.multiple_of(step * 16, 16), 16)
            low_w[rows, :] = (scores[rows, :] * inverse).astype(jnp.bfloat16)
            low_s[rows, :] = (slopes[rows, :] * inverse * (dweights[rows, :] - delta)).astype(
                jnp.bfloat16
            )
            return carry

        lax.fori_loop(0, PAIR // 16, finish, 0, unroll=21)
        rows_grad = dot(low_s[...], keys[window, :], ((0,), (0,))).astype(jnp.bfloat16)
        for z in range(2):
            for n in range(2):
                first = z * 64 + n * PIECE
                query_grad[pair * 2 + z, :, n * 256 : n * 256 + 256] = rows_grad[
                    first : first + PIECE, :
                ]
        for acc, terms in (
            (key_acc, dot(low_s[...], queries, ((1,), (0,)))),
            (value_acc, dot(low_w[...], grads, ((1,), (0,)))),
        ):
            if pair == 0:
                acc[window, :] = terms
            else:
                acc[pl.ds(pl.multiple_of(low, PIECE), SHARED), :] += terms[0:SHARED, :]
                acc[pl.ds(pl.multiple_of(low + SHARED, PIECE), 256), :] = terms[SHARED:PAIR, :]

    def take(target, idx, rows):
        target[idx, :, 0:256] = key_acc[rows, :].astype(target.dtype)
        target[idx, :, 256:512] = value_acc[rows, :].astype(target.dtype)

    for idx in range(16):
        take(theirs_reach, idx, reach_rows(place, idx, True))
        take(mine_reach, idx, reach_rows(place, idx, False))
    for z in range(8):
        take(theirs, z, piece_rows(place, 512, z, False, True))
        take(mine, z, piece_rows(place, 512, z, False, False))


def sum_reach_kernel(mine, received, across, before, before_across):
    for idx in range(16):
        total = (mine[idx] + received[idx].astype(jnp.float32)).astype(jnp.bfloat16)
        if idx < 8:
            across[idx] = total
        elif idx < 12:
            before[idx - 8] = total
        else:
            before_across[idx - 12] = total


def sum_own_kernel(query_grad, mine, partner, across, after, after_across, out):
    out[:, :, 0:512] = query_grad[...]
    for z in range(8):
        total = mine[z] + partner[z].astype(jnp.float32) + across[z].astype(jnp.float32)
        if z >= 4:
            total = total + after[z - 4].astype(jnp.float32)
            total = total + after_across[z - 4].astype(jnp.float32)
        out[z, :, 512:1024] = total.astype(jnp.bfloat16)


def unpack_kernel(pieces, q_ref, k_ref, v_ref):
    for head in range(8):
        q_ref[:, head * 512 : head * 512 + 512] = pieces[head, :, 0:512]
        k_ref[:, head * 256 : head * 256 + 256] = pieces[head, :, 512:768]
        v_ref[:, head * 256 : head * 256 + 256] = pieces[head, :, 768:1024]


def struct(*dims, dtype=jnp.bfloat16):
    return jax.ShapeDtypeStruct(dims, dtype)


def exchange(value):
    return lax.all_to_all(value, "z", split_axis=0, concat_axis=0, tiled=True)


LINE, CROSS = ("y", "xlo"), ("y", "xlo", "xhi")


def shards(query_proj, key_proj, value_proj, out_grad):
    y, xlo, xhi, core = (lax.axis_index(name) for name in ("y", "xlo", "xhi", "core"))
    place = jnp.stack([xhi, core, y * 2 + xlo]).astype(jnp.int32)
    own = exchange(pack(key_proj, value_proj, limit=60))
    across = lax.ppermute(own, "xhi", SWAP)
    before = lax.ppermute(own[4:8], LINE, line_perm(1))
    before_across = lax.ppermute(own[4:8], CROSS, cross_perm(1))
    partner = lax.ppermute(own, "core", SWAP)
    qg = exchange(pack(query_proj, out_grad))
    reach = lax.ppermute(jnp.concatenate([across, before, before_across], axis=0), "core", SWAP)
    f32, bf16 = jnp.float32, jnp.bfloat16
    query_grad, mine, mine_reach, theirs, theirs_reach = vmem_call(
        attention_kernel,
        (
            struct(8, 32, 512),
            struct(8, 32, 512, dtype=f32),
            struct(16, 32, 512, dtype=f32),
            struct(8, 32, 512),
            struct(16, 32, 512),
        ),
        (place, qg, own, partner, across, before, before_across, reach),
        scratch=[
            pltpu.VMEM((512, 256), bf16),
            pltpu.VMEM((512, 256), bf16),
            pltpu.VMEM((SPAN, 256), bf16),
            pltpu.VMEM((SPAN, 256), bf16),
            pltpu.VMEM((PAIR, 128), f32),
            pltpu.VMEM((PAIR, 128), f32),
            pltpu.VMEM((PAIR, 128), f32),
            pltpu.VMEM((PAIR, 128), bf16),
            pltpu.VMEM((PAIR, 128), bf16),
            pltpu.VMEM((SPAN, 256), f32),
            pltpu.VMEM((SPAN, 256), f32),
        ],
        flops=2 * 5 * 4 * PAIR * 128 * 256,
        transcendentals=2 * 4 * PAIR * 128,
        places=1,
    )
    reach_received = lax.ppermute(theirs_reach, "core", SWAP)
    received = lax.ppermute(theirs, "core", SWAP)
    across, before, before_across = vmem_call(
        sum_reach_kernel,
        (struct(8, 32, 512), struct(4, 32, 512), struct(4, 32, 512)),
        (mine_reach, reach_received),
    )
    across = lax.ppermute(across, "xhi", SWAP)
    after = lax.ppermute(before, LINE, line_perm(-1))
    after_across = lax.ppermute(before_across, CROSS, cross_perm(-1))
    pieces = exchange(
        vmem_call(
            sum_own_kernel,
            struct(8, 32, 1024),
            (query_grad, mine, received, across, after, after_across),
        ),
    )
    return vmem_call(
        unpack_kernel, (struct(32, 4096), struct(32, 2048), struct(32, 2048)), (pieces,)
    )


def solution(mesh):
    fine = Mesh(mesh.devices.reshape(SIZES), NAMES)
    spec = P(NAMES, None)
    return jax.shard_map(
        shards, mesh=fine, in_specs=(spec,) * 4, out_specs=(spec,) * 3, check_vma=False
    )
```

```python
import functools
import math

import jax
import jax.numpy as jnp
from jax import lax
from jax.experimental import pallas as pl
from jax.experimental.pallas import tpu as pltpu
from jax.sharding import Mesh, PartitionSpec as P


HEAD_DIM = 256
SOFTCAP = 50.0
SCALE = 1.0 / math.sqrt(HEAD_DIM)
NAMES = ("y", "xlo", "z", "xhi", "core")
SIZES = (8, 2, 8, 2, 2)
LINES = 16
PIECE = 32
PAIR = 672
SHARED = PAIR - 256
SPAN = 1536


def line_perm(steps):
    return [
        (line, line + steps) for line in range(max(0, -steps), min(LINES, LINES - steps))
    ]


def cross_perm(steps):
    return [
        (source * 2 + xhi, target * 2 + 1 - xhi)
        for source, target in line_perm(steps)
        for xhi in range(2)
    ]


SWAP = [(0, 1), (1, 0)]


def vmem_call(kernel, out_shape, args, scratch=(), flops=0, transcendentals=0, places=0, away=0, limit=16):
    spec = pl.BlockSpec(memory_space=pltpu.VMEM)
    remote = pl.BlockSpec(memory_space=pl.ANY)
    moved = sum(a.size * a.dtype.itemsize for a in jax.tree.leaves((args, out_shape)))
    return pl.pallas_call(
        kernel,
        out_shape=out_shape,
        in_specs=[pl.BlockSpec(memory_space=pltpu.SMEM)] * places
        + [remote] * away
        + [spec] * (len(args) - places - away),
        out_specs=jax.tree.map(lambda _: spec, out_shape),
        scratch_shapes=list(scratch),
        compiler_params=pltpu.CompilerParams(
            vmem_limit_bytes=limit << 20
        ),
        cost_estimate=pl.CostEstimate(
            flops=flops, bytes_accessed=moved, transcendentals=transcendentals
        ),
    )(*args)


def pack_kernel(width, left, right, out, sems):
    copies = []
    for head in range(8):
        for side, source in enumerate((left, right)):
            copies.append(
                pltpu.make_async_copy(
                    source.at[:, head * width : head * width + width],
                    out.at[head, :, side * width : side * width + width],
                    sems.at[head * 2 + side],
                )
            )
    for copy in copies:
        copy.start()
    for copy in copies:
        copy.wait()


def pack(left, right, limit=16):
    width = left.shape[1] // 8
    return vmem_call(
        functools.partial(pack_kernel, width),
        struct(8, 32, 2 * width),
        (left, right),
        scratch=[pltpu.SemaphoreType.DMA((16,))],
        away=2,
        limit=limit,
    )


def dot(left, right, contract):
    return lax.dot_general(
        left, right, (contract, ((), ())), preferred_element_type=jnp.float32
    )


def piece_rows(place, base, chunk, other_x, other_c):
    xhi = 1 - place[0] if other_x else place[0]
    core = 1 - place[1] if other_c else place[1]
    return pl.ds(pl.multiple_of(base + chunk * 128 + xhi * 64 + core * PIECE, PIECE), PIECE)


def reach_rows(place, idx, other_c):
    if idx < 8:
        return piece_rows(place, 512, idx, True, other_c)
    return piece_rows(place, 0, idx % 4, idx >= 12, other_c)


def attention_kernel(place, qg, own, partner, across, before, before_across, reach, *refs):
    query_grad, mine, mine_reach, theirs, theirs_reach = refs[:5]
    qs, gs, keys, values, scores, dweights, slopes, low_w, low_s, key_acc, value_acc = refs[5:]

    def put(rows, piece):
        keys[rows, :] = piece[:, 0:256]
        values[rows, :] = piece[:, 256:512]

    for z in range(8):
        put(piece_rows(place, 512, z, False, False), own[z])
        put(piece_rows(place, 512, z, False, True), partner[z])
        put(piece_rows(place, 512, z, True, False), across[z])
    for z in range(4):
        put(piece_rows(place, 0, z, False, False), before[z])
        put(piece_rows(place, 0, z, True, False), before_across[z])
    for idx in range(16):
        put(reach_rows(place, idx, True), reach[idx])
    for z in range(8):
        for n in range(2):
            rows = slice(z * 64 + n * PIECE, z * 64 + n * PIECE + PIECE)
            qs[rows, :] = qg[z, :, n * 256 : n * 256 + 256]
            gs[rows, :] = qg[z, :, 512 + n * 256 : 768 + n * 256]
    for acc in (key_acc, value_acc):
        acc[0:96, :] = jnp.zeros((96, 256), jnp.float32)
        acc[1440:SPAN, :] = jnp.zeros((96, 256), jnp.float32)
    offset = place[0] * 64 + place[1] * PIECE
    column = lax.broadcasted_iota(jnp.int32, (16, 128), 1)
    token = (column // 64) * 128 + (column & 31)
    stop = token + 512
    key_row = lax.broadcasted_iota(jnp.int32, (16, 128), 0)
    for pair in range(4):
        low = 256 * pair + offset
        window = pl.ds(pl.multiple_of(low, PIECE), PAIR)
        queries = qs[pair * 128 : pair * 128 + 128, :]
        grads = gs[pair * 128 : pair * 128 + 128, :]
        scores[...] = dot(keys[window, :], queries, ((1,), (1,)))
        dweights[...] = dot(values[window, :], grads, ((1,), (1,)))
        start = jnp.maximum(token + 1, jnp.where(place[2] == 0, 512 - low, 0))

        def sums(allowed, step, carry):
            total, delta = carry
            rows = pl.ds(pl.multiple_of(step * 16, 16), 16)
            bent = jnp.tanh(scores[rows, :] * (SCALE / SOFTCAP))
            weight = jnp.where(allowed(key_row + step * 16), jnp.exp(SOFTCAP * bent), 0.0)
            scores[rows, :] = weight
            total = total + weight
            delta = delta + weight * dweights[rows, :]
            slopes[rows, :] = weight * (SCALE - SCALE * (bent * bent))
            return total, delta

        zero = jnp.zeros((16, 128), jnp.float32)
        early = functools.partial(sums, lambda row: row >= start)
        late = functools.partial(sums, lambda row: row <= stop)
        total, delta = lax.fori_loop(0, 32, early, (zero, zero), unroll=16)
        total, delta = lax.fori_loop(32, PAIR // 16, late, (total, delta), unroll=10)
        inverse = 1.0 / jnp.sum(total, axis=0, keepdims=True)
        delta = jnp.sum(delta, axis=0, keepdims=True) * inverse
        inverse = jnp.broadcast_to(inverse, (16, 128))
        delta = jnp.broadcast_to(delta, (16, 128))

        def finish(step, carry):
            rows = pl.ds(pl.multiple_of(step * 16, 16), 16)
            low_w[rows, :] = (scores[rows, :] * inverse).astype(jnp.bfloat16)
            low_s[rows, :] = (slopes[rows, :] * inverse * (dweights[rows, :] - delta)).astype(
                jnp.bfloat16
            )
            return carry

        lax.fori_loop(0, PAIR // 16, finish, 0, unroll=21)
        rows_grad = dot(low_s[...], keys[window, :], ((0,), (0,))).astype(jnp.bfloat16)
        for z in range(2):
            for n in range(2):
                first = z * 64 + n * PIECE
                query_grad[pair * 2 + z, :, n * 256 : n * 256 + 256] = rows_grad[
                    first : first + PIECE, :
                ]
        for acc, terms in (
            (key_acc, dot(low_s[...], queries, ((1,), (0,)))),
            (value_acc, dot(low_w[...], grads, ((1,), (0,)))),
        ):
            if pair == 0:
                acc[window, :] = terms
            else:
                acc[pl.ds(pl.multiple_of(low, PIECE), SHARED), :] += terms[0:SHARED, :]
                acc[pl.ds(pl.multiple_of(low + SHARED, PIECE), 256), :] = terms[SHARED:PAIR, :]

    def take(target, idx, rows):
        target[idx, :, 0:256] = key_acc[rows, :].astype(target.dtype)
        target[idx, :, 256:512] = value_acc[rows, :].astype(target.dtype)

    for idx in range(16):
        take(theirs_reach, idx, reach_rows(place, idx, True))
        take(mine_reach, idx, reach_rows(place, idx, False))
    for z in range(8):
        take(theirs, z, piece_rows(place, 512, z, False, True))
        take(mine, z, piece_rows(place, 512, z, False, False))


def sum_reach_kernel(mine, received, across, before, before_across):
    for idx in range(16):
        total = (mine[idx] + received[idx].astype(jnp.float32)).astype(jnp.bfloat16)
        if idx < 8:
            across[idx] = total
        elif idx < 12:
            before[idx - 8] = total
        else:
            before_across[idx - 12] = total


def sum_own_kernel(mine, partner, across, after, after_across, out):
    for z in range(8):
        total = mine[z] + partner[z].astype(jnp.float32) + across[z].astype(jnp.float32)
        if z >= 4:
            total = total + after[z - 4].astype(jnp.float32)
            total = total + after_across[z - 4].astype(jnp.float32)
        out[z] = total.astype(jnp.bfloat16)


def unpack_q_kernel(pieces, q_ref):
    for head in range(8):
        q_ref[:, head * 512 : head * 512 + 512] = pieces[head]


def unpack_kv_kernel(pieces, k_ref, v_ref):
    for head in range(8):
        k_ref[:, head * 256 : head * 256 + 256] = pieces[head, :, 0:256]
        v_ref[:, head * 256 : head * 256 + 256] = pieces[head, :, 256:512]


def struct(*dims, dtype=jnp.bfloat16):
    return jax.ShapeDtypeStruct(dims, dtype)


def exchange(value):
    return lax.all_to_all(value, "z", split_axis=0, concat_axis=0, tiled=True)


LINE, CROSS = ("y", "xlo"), ("y", "xlo", "xhi")


def shards(query_proj, key_proj, value_proj, out_grad):
    y, xlo, xhi, core = (lax.axis_index(name) for name in ("y", "xlo", "xhi", "core"))
    place = jnp.stack([xhi, core, y * 2 + xlo]).astype(jnp.int32)
    own = exchange(pack(key_proj, value_proj, limit=60))
    across = lax.ppermute(own, "xhi", SWAP)
    before = lax.ppermute(own[4:8], LINE, line_perm(1))
    before_across = lax.ppermute(own[4:8], CROSS, cross_perm(1))
    partner = lax.ppermute(own, "core", SWAP)
    qg = exchange(pack(query_proj, out_grad))
    reach = lax.ppermute(jnp.concatenate([across, before, before_across], axis=0), "core", SWAP)
    f32, bf16 = jnp.float32, jnp.bfloat16
    query_grad, mine, mine_reach, theirs, theirs_reach = vmem_call(
        attention_kernel,
        (
            struct(8, 32, 512),
            struct(8, 32, 512, dtype=f32),
            struct(16, 32, 512, dtype=f32),
            struct(8, 32, 512),
            struct(16, 32, 512),
        ),
        (place, qg, own, partner, across, before, before_across, reach),
        scratch=[
            pltpu.VMEM((512, 256), bf16),
            pltpu.VMEM((512, 256), bf16),
            pltpu.VMEM((SPAN, 256), bf16),
            pltpu.VMEM((SPAN, 256), bf16),
            pltpu.VMEM((PAIR, 128), f32),
            pltpu.VMEM((PAIR, 128), f32),
            pltpu.VMEM((PAIR, 128), f32),
            pltpu.VMEM((PAIR, 128), bf16),
            pltpu.VMEM((PAIR, 128), bf16),
            pltpu.VMEM((SPAN, 256), f32),
            pltpu.VMEM((SPAN, 256), f32),
        ],
        flops=2 * 5 * 4 * PAIR * 128 * 256,
        transcendentals=2 * 4 * PAIR * 128,
        places=1,
    )
    reach_received = lax.ppermute(theirs_reach, "core", SWAP)
    received = lax.ppermute(theirs, "core", SWAP)
    across, before, before_across = vmem_call(
        sum_reach_kernel,
        (struct(8, 32, 512), struct(4, 32, 512), struct(4, 32, 512)),
        (mine_reach, reach_received),
    )
    across = lax.ppermute(across, "xhi", SWAP)
    after = lax.ppermute(before, LINE, line_perm(-1))
    after_across = lax.ppermute(before_across, CROSS, cross_perm(-1))
    query_out = exchange(query_grad)
    kv_out = exchange(
        vmem_call(
            sum_own_kernel,
            struct(8, 32, 512),
            (mine, received, across, after, after_across),
        ),
    )
    key_out, value_out = vmem_call(
        unpack_kv_kernel, (struct(32, 2048), struct(32, 2048)), (kv_out,)
    )
    query_low = vmem_call(unpack_q_kernel, struct(32, 4096), (query_out,))
    return query_low, key_out, value_out


def solution(mesh):
    fine = Mesh(mesh.devices.reshape(SIZES), NAMES)
    spec = P(NAMES, None)
    return jax.shard_map(
        shards, mesh=fine, in_specs=(spec,) * 4, out_specs=(spec,) * 3, check_vma=False
    )
```
